32 devices in a mesh: row: 16 (over z, y, core), col: 2 (over x).
Axes of the slice: x: 2, y: 2, z: 4, core: 2. Of those that a mesh axis runs over, the one named last changes fastest.
Arguments:
- source: float32 [4096, 2048], P('row', 'col'), may hold values from 0.25 to 4
- boxes_a: float32 [16, 8, 512, 512], P('row', 'col'), may hold values from 0.25 to 4
- shifts_a: int32 [16, 8, 2], P('row', 'col'), may hold values from -128 to -1
- widths_a: int32 [16, 8, 2], P('row', 'col'), may hold values from 256 to 512
- boxes_b: float32 [16, 8, 512, 512], P('row', 'col'), may hold values from 0.25 to 4
- shifts_b: int32 [16, 8, 2], P('row', 'col'), may hold values from -128 to -1
- widths_b: int32 [16, 8, 2], P('row', 'col'), may hold values from 256 to 512
Outputs:
- smoothed: float32 [4096, 2048], P('row', 'col')
The draws below stay inside these ranges and needn't reach their ends.
Inputs may be any that keep to these rules, and one draw needn't show every extreme that they name: `shifts_a`: first entry: rows, second: columns. `widths_a`: first entry: rows, second: columns. `shifts_b`: first entry: rows, second: columns. `widths_b`: first entry: rows, second: columns.
All inputs are finite; a program needn't handle non-finite values.
Results may differ from the reference program's by a relative error of at most 0.0003.
Values sent between devices are 32-bit elements; how exact they have to be, the bound alone decides.
A program may use at most 64 MiB of HBM per device.

```python
import math
import jax
import jax.numpy as jnp
from jax import lax

S = 256
BOX = 512
ITERS = 3
RADIUS = 8
CELL_ROWS = 16
CELL_COLS = 8
NR = 4096
NC = 2048


def place_ends(array, stream_key, least, largest):
    index_at = [jax.random.randint(jax.random.fold_in(stream_key, axis), (), 0, length) for axis, length in enumerate(array.shape)]
    widest = array.shape.index(max(array.shape))
    neighbour = index_at[:widest] + [(index_at[widest] + 1) % array.shape[widest]] + index_at[widest + 1:]
    return array.at[tuple(index_at)].set(least).at[tuple(neighbour)].set(largest)


def steps_of(stream_key, extent, pieces, least, largest):
    level, own = 1.0, jax.random.fold_in(stream_key, 6)
    for dim, parts in pieces:
        steps = jnp.exp(jax.random.uniform(jax.random.fold_in(own, dim), (parts,), jnp.float32, least / len(pieces), largest / len(pieces)))
        level = level * jnp.repeat(steps, extent[dim] // parts).reshape([-1 if axis == dim else 1 for axis in range(len(extent))])
    return level


def setup_inputs(seed: int = 0) -> dict:
    arg_keys = jax.random.split(jax.random.key(seed), 8)
    return {
        "source": jnp.clip(jnp.exp(math.log(4.0) - 2.7725887 * jax.random.uniform(arg_keys[0], (NR, NC), jnp.float32) ** steps_of(arg_keys[0], (NR, NC), ((0, 16), (1, 2)), -0.2, 0.2)), 0.25, 4.0),
        "boxes_a": jnp.clip(jnp.exp(math.log(4.0) - 2.7725887 * jax.random.uniform(arg_keys[1], (CELL_ROWS, CELL_COLS, BOX, BOX), jnp.float32) ** steps_of(arg_keys[1], (CELL_ROWS, CELL_COLS, BOX, BOX), ((0, 16), (1, 2)), -0.2, 0.2)), 0.25, 4.0),
        "shifts_a": place_ends(jax.random.randint(arg_keys[2], (CELL_ROWS, CELL_COLS, 2), 0 - S // 2, 0), jax.random.fold_in(arg_keys[2], 1), 0 - S // 2, -1).astype(jnp.int32),
        "widths_a": place_ends(jax.random.randint(arg_keys[3], (CELL_ROWS, CELL_COLS, 2), S, 2 * S + 1), jax.random.fold_in(arg_keys[3], 1), S, 2 * S).astype(jnp.int32),
        "boxes_b": jnp.clip(jnp.exp(math.log(4.0) - 2.7725887 * jax.random.uniform(arg_keys[4], (CELL_ROWS, CELL_COLS, BOX, BOX), jnp.float32) ** steps_of(arg_keys[4], (CELL_ROWS, CELL_COLS, BOX, BOX), ((0, 16), (1, 2)), -0.2, 0.2)), 0.25, 4.0),
        "shifts_b": place_ends(jax.random.randint(arg_keys[5], (CELL_ROWS, CELL_COLS, 2), 0 - S // 2, 0), jax.random.fold_in(arg_keys[5], 1), 0 - S // 2, -1).astype(jnp.int32),
        "widths_b": place_ends(jax.random.randint(arg_keys[6], (CELL_ROWS, CELL_COLS, 2), S, 2 * S + 1), jax.random.fold_in(arg_keys[6], 1), S, 2 * S).astype(jnp.int32),
    }


kernel_eps = 0.05
blur_sigma = 2.0


def table(patch_displacement):
    rows = jnp.arange(S, dtype=jnp.int32)
    cols = jnp.arange(BOX, dtype=jnp.int32)
    dist = (patch_displacement + cols[None, :] - rows[:, None]).astype(jnp.float32) / S
    return jnp.exp(-dist * dist / kernel_eps).astype(jnp.bfloat16)


def masked(patch_rectangle, patch_extent):
    index = jnp.arange(BOX, dtype=jnp.int32)
    keep_rows = (index < patch_extent[0]).astype(jnp.float32)
    keep_cols = (index < patch_extent[1]).astype(jnp.float32)
    return patch_rectangle * keep_rows[:, None] * keep_cols[None, :]


def apply_back(horizontal_kernel_grid, vertical_kernel_grid, multiplier_array):
    inner = jnp.dot(horizontal_kernel_grid.T, multiplier_array.astype(jnp.bfloat16), preferred_element_type=jnp.float32)
    return jnp.dot(inner.astype(jnp.bfloat16), vertical_kernel_grid, preferred_element_type=jnp.float32)


def apply_fwd(horizontal_kernel_grid, vertical_kernel_grid, multiplier_array):
    inner = jnp.dot(horizontal_kernel_grid, multiplier_array.astype(jnp.bfloat16), preferred_element_type=jnp.float32)
    return jnp.dot(inner.astype(jnp.bfloat16), vertical_kernel_grid.T, preferred_element_type=jnp.float32)


def entropic_transport_iterate(probability_measure, patch_rectangle, patch_displacement, patch_extent, initial_corner_index):
    horizontal_kernel_grid = table(patch_displacement[0])
    vertical_kernel_grid = table(patch_displacement[1])
    target = masked(patch_rectangle, patch_extent)
    multiplier_array = initial_corner_index
    lagrange_multiplier_field = target
    for step in range(ITERS):
        lagrange_multiplier_field = target / apply_back(horizontal_kernel_grid, vertical_kernel_grid, multiplier_array)
        multiplier_array = probability_measure / apply_fwd(horizontal_kernel_grid, vertical_kernel_grid, lagrange_multiplier_field)
    return multiplier_array, lagrange_multiplier_field, horizontal_kernel_grid, vertical_kernel_grid


def section_first(probability_measure, patch_rectangle, patch_displacement, patch_extent):
    multiplier_array, lagrange_multiplier_field, horizontal_kernel_grid, vertical_kernel_grid = entropic_transport_iterate(probability_measure, patch_rectangle, patch_displacement, patch_extent, jnp.ones_like(probability_measure))
    return multiplier_array


def section_second(probability_measure, initial_corner_index, patch_rectangle, patch_displacement, patch_extent):
    multiplier_array, lagrange_multiplier_field, horizontal_kernel_grid, vertical_kernel_grid = entropic_transport_iterate(probability_measure, patch_rectangle, patch_displacement, patch_extent, initial_corner_index)
    return lagrange_multiplier_field * apply_back(horizontal_kernel_grid, vertical_kernel_grid, multiplier_array)


def blur_pairs():
    raw = [math.exp(-(step * step) / (2.0 * blur_sigma * blur_sigma)) for step in range(-RADIUS, RADIUS + 1)]
    total = sum(raw)
    return [(step, raw[step + RADIUS] / total) for step in range(-RADIUS, RADIUS + 1)]


def to_cells(field):
    return field.reshape(CELL_ROWS, S, CELL_COLS, S).transpose(0, 2, 1, 3)


def from_cells(cells):
    return cells.transpose(0, 2, 1, 3).reshape(NR, NC)


def reference(source, boxes_a, shifts_a, widths_a, boxes_b, shifts_b, widths_b):
    half = S // 2
    first = lax.map(lambda row: jax.vmap(section_first)(*row), (to_cells(source), boxes_a, shifts_a, widths_a))
    u_first = from_cells(first)
    u_moved = jnp.roll(u_first, (-half, -half), (0, 1))
    mass_moved = jnp.roll(source, (-half, -half), (0, 1))
    plans = lax.map(lambda row: jax.vmap(section_second)(*row),
                    (to_cells(mass_moved), to_cells(u_moved), boxes_b, shifts_b, widths_b))
    canvas = jnp.zeros((NR + 2 * S, NC + 2 * S), jnp.float32)

    def place(index, canvas):
        cell_row = index // CELL_COLS
        cell_col = index % CELL_COLS
        plan = plans[cell_row, cell_col]
        top = (cell_row * S + half + shifts_b[cell_row, cell_col, 0]).astype(jnp.int32)
        left = (cell_col * S + half + shifts_b[cell_row, cell_col, 1]).astype(jnp.int32)
        region = lax.dynamic_slice(canvas, (top, left), (BOX, BOX))
        return lax.dynamic_update_slice(canvas, region + plan, (top, left))

    canvas = lax.fori_loop(0, CELL_ROWS * CELL_COLS, place, canvas)
    folded = canvas[:NR].at[:2 * S].add(canvas[NR:])
    gathered = folded[:, :NC].at[:, :2 * S].add(folded[:, NC:])
    row_smooth = jnp.zeros_like(gathered)
    for step, weight in blur_pairs():
        row_smooth = row_smooth + weight * jnp.roll(gathered, -step, 0)
    smoothed = jnp.zeros_like(gathered)
    for step, weight in blur_pairs():
        smoothed = smoothed + weight * jnp.roll(row_smooth, -step, 1)
    return smoothed
```

```python
import functools
import math

import jax
import jax.numpy as jnp
from jax import lax
from jax.experimental import pallas as pl
from jax.experimental.pallas import tpu as pltpu
from jax.sharding import PartitionSpec as P

S = 256
BOX = 512
ITERS = 3
RADIUS = 8
LANES = 128
HALF = S // 2
DOWN2 = HALF + RADIUS
TALL = RADIUS + 2 * S + DOWN2

kernel_eps = 0.05
blur_sigma = 2.0
blur_total = sum(
    math.exp(-(d * d) / (2.0 * blur_sigma * blur_sigma)) for d in range(-RADIUS, RADIUS + 1)
)


def gauss(offset, shape, box_dim):
    k = lax.broadcasted_iota(jnp.int32, shape, box_dim)
    p = lax.broadcasted_iota(jnp.int32, shape, 1 - box_dim)
    dist = (offset + k - p).astype(jnp.float32) * (1.0 / S)
    return jnp.exp(dist * dist * (-1.0 / kernel_eps)).astype(jnp.bfloat16)


def blur_weight(d):
    f = d.astype(jnp.float32)
    w = jnp.exp(f * f * (-1.0 / (2.0 * blur_sigma * blur_sigma))) * (1.0 / blur_total)
    return jnp.where(jnp.abs(d) <= RADIUS, w, 0.0)


def split(x):
    hi = x.astype(jnp.bfloat16)
    return hi, (x - hi.astype(jnp.float32)).astype(jnp.bfloat16)


def dot(a, b):
    return jnp.dot(a, b, preferred_element_type=jnp.float32)


def dot_t(a, b):
    return lax.dot_general(a, b, (((1,), (1,)), ((), ())), preferred_element_type=jnp.float32)


def dot_split(a, b):
    (ah, al), (bh, bl) = a, b
    return dot(ah, bh) + (dot(ah, bl) + dot(al, bh))


def bf(x):
    return x.astype(jnp.bfloat16)


def target_of(box_ref, height, width):
    rows = lax.broadcasted_iota(jnp.int32, (BOX, BOX), 0)
    cols = lax.broadcasted_iota(jnp.int32, (BOX, BOX), 1)
    return jnp.where((rows < height) & (cols < width), box_ref[0, 0], 0.0)


def kernel_a(shift_ref, width_ref, a_ref, box_ref, u_ref, tgt):
    j = pl.program_id(0)
    o_r, o_c = shift_ref[j, 0], shift_ref[j, 1]
    kr = gauss(o_r, (S, BOX), 1)
    krt = gauss(o_r, (BOX, S), 0)
    kc = gauss(o_c, (S, BOX), 1)
    tgt[...] = target_of(box_ref, width_ref[j, 0], width_ref[j, 1])
    a = a_ref[...]
    in_r = bf(jnp.sum(krt.astype(jnp.float32), axis=1, keepdims=True)).astype(jnp.float32)
    in_c = jnp.sum(kc.astype(jnp.float32), axis=0, keepdims=True)
    back = in_r * in_c
    for step in range(ITERS):
        v = bf(tgt[...] / back)
        u = a / dot_t(bf(dot(kr, v)), kc)
        if step < ITERS - 1:
            back = dot(bf(dot(krt, bf(u))), kc)
    u_ref[...] = u


def kernel_b(per_dev, shift_ref, width_ref, a_ref, u_ref, box_ref, up_ref, own_ref, d1_ref, d2_ref, tgt, canvas):
    j = pl.program_id(0)
    o_r, o_c = shift_ref[j, 0], shift_ref[j, 1]
    wide = canvas.shape[1]

    @pl.when(j == 0)
    def _():
        canvas[...] = jnp.zeros_like(canvas)

    kr = gauss(o_r, (S, BOX), 1)
    krt = gauss(o_r, (BOX, S), 0)
    kc = gauss(o_c, (S, BOX), 1)
    tgt[...] = target_of(box_ref, width_ref[j, 0], width_ref[j, 1])
    a = a_ref[...]
    u = u_ref[...]
    for step in range(ITERS):
        back = dot(bf(dot(krt, bf(u))), kc)
        v = tgt[...] / back
        u = a / dot_t(bf(dot(kr, bf(v))), kc)
    plan = v * dot(bf(dot(krt, bf(u))), kc)

    y = lax.broadcasted_iota(jnp.int32, (TALL, BOX), 0) - RADIUS
    k = lax.broadcasted_iota(jnp.int32, (TALL, BOX), 1)
    rowed = dot_split(split(blur_weight(HALF + o_r + k - y)), split(plan))
    s = HALF + o_c
    lane = lax.broadcasted_iota(jnp.int32, (TALL, LANES), 1)
    turned = [
        pltpu.roll(rowed[:, t * LANES : (t + 1) * LANES], s, 1) for t in range(BOX // LANES)
    ]
    zero = jnp.zeros((TALL, LANES), jnp.float32)
    for t in range(BOX // LANES + 1):
        left = turned[t - 1] if t > 0 else zero
        here = turned[t] if t < BOX // LANES else zero
        at = pl.ds(pl.multiple_of(j * S + t * LANES, LANES), LANES)
        canvas[:, at] += jnp.where(lane < s, left, here)

    @pl.when(j == per_dev - 1)
    def _():
        n = lax.broadcasted_iota(jnp.int32, (2 * S, S), 0)
        m = lax.broadcasted_iota(jnp.int32, (2 * S, S), 1)
        band = split(blur_weight(n - LANES - m))
        for t in range(wide // S):
            lo, hi = t * S - LANES, t * S + S + LANES
            if lo < 0:
                near = jnp.concatenate([canvas[:, wide + lo :], canvas[:, :hi]], axis=1)
            elif hi > wide:
                near = jnp.concatenate([canvas[:, lo:], canvas[:, : hi - wide]], axis=1)
            else:
                near = canvas[:, lo:hi]
            out = dot_split(split(near), band)
            at = slice(t * S, (t + 1) * S)
            up_ref[:, at] = out[:RADIUS]
            own_ref[:, at] = out[RADIUS : RADIUS + S]
            d1_ref[:, at] = out[RADIUS + S : RADIUS + 2 * S]
            d2_ref[:, at] = out[RADIUS + 2 * S :]


def cell_block():
    return pl.BlockSpec((S, S), lambda j, *_: (0, j))


def box_block():
    return pl.BlockSpec((1, 1, BOX, BOX), lambda j, *_: (0, j, 0, 0))


def moved_by(array, axis, by):
    length = lax.axis_size(axis)
    return lax.ppermute(array, axis, [(i, (i + by) % length) for i in range(length)])


def shifted(field):
    below = moved_by(field[:HALF], "row", -1)
    rowset = jnp.concatenate([field[HALF:], below], axis=0)
    beside = moved_by(rowset[:, :HALF], "col", -1)
    return jnp.concatenate([rowset[:, HALF:], beside], axis=1)


def on_device(source, boxes_a, shifts_a, widths_a, boxes_b, shifts_b, widths_b):
    cols = source.shape[1]
    per_dev = cols // S
    wide = cols + 2 * S
    params = pltpu.CompilerParams(vmem_limit_bytes=56 * 1024 * 1024)

    u_first = pl.pallas_call(
        kernel_a,
        grid_spec=pltpu.PrefetchScalarGridSpec(
            num_scalar_prefetch=2,
            grid=(per_dev,),
            in_specs=[cell_block(), box_block()],
            out_specs=cell_block(),
            scratch_shapes=[pltpu.VMEM((BOX, BOX), jnp.float32)],
        ),
        out_shape=jax.ShapeDtypeStruct((S, cols), jnp.float32),
        compiler_params=params,
        name="aligned",
    )(shifts_a[0], widths_a[0], source, boxes_a)

    whole = lambda h: pl.BlockSpec((h, wide), lambda j, *_: (0, 0))
    up, own, down1, down2 = pl.pallas_call(
        functools.partial(kernel_b, per_dev),
        grid_spec=pltpu.PrefetchScalarGridSpec(
            num_scalar_prefetch=2,
            grid=(per_dev,),
            in_specs=[cell_block(), cell_block(), box_block()],
            out_specs=[whole(h) for h in (RADIUS, S, S, DOWN2)],
            scratch_shapes=[
                pltpu.VMEM((BOX, BOX), jnp.float32),
                pltpu.VMEM((TALL, wide), jnp.float32),
            ],
        ),
        out_shape=[jax.ShapeDtypeStruct((h, wide), jnp.float32) for h in (RADIUS, S, S, DOWN2)],
        compiler_params=params,
        name="shifted",
    )(shifts_b[0], widths_b[0], shifted(source), shifted(u_first), boxes_b)

    total = own + moved_by(down1, "row", 1)
    total = total.at[:DOWN2].add(moved_by(down2, "row", 2))
    total = total.at[S - RADIUS :].add(moved_by(up, "row", -1))
    spill = total[:, cols:]
    x = lax.broadcasted_iota(jnp.int32, (1, 2 * S), 1)
    ahead = moved_by(spill, "col", 1)
    behind = ahead if lax.axis_size("col") == 2 else moved_by(spill[:, -LANES:], "col", -1)
    ahead = jnp.where(x < 2 * S - RADIUS, ahead, 0.0)
    behind = jnp.where(x[:, -LANES:] >= 2 * S - RADIUS, behind[:, -LANES:], 0.0)
    out = total[:, :cols].at[:, : 2 * S].add(ahead)
    return out.at[:, cols - LANES :].add(behind)


def solution(mesh):
    return jax.shard_map(
        on_device,
        mesh=mesh,
        in_specs=(
            P("row", "col"),
            P("row", "col", None, None),
            P("row", "col", None),
            P("row", "col", None),
            P("row", "col", None, None),
            P("row", "col", None),
            P("row", "col", None),
        ),
        out_specs=P("row", "col"),
        check_vma=False,
    )
```

```python
import functools
import math

import jax
import jax.numpy as jnp
from jax import lax
from jax.experimental import pallas as pl
from jax.experimental.pallas import tpu as pltpu
from jax.sharding import PartitionSpec as P

S = 256
BOX = 512
ITERS = 3
RADIUS = 8
LANES = 128
HALF = S // 2
DOWN2 = HALF + RADIUS
TALL = RADIUS + 2 * S + DOWN2

kernel_eps = 0.05
blur_sigma = 2.0
blur_total = sum(
    math.exp(-(d * d) / (2.0 * blur_sigma * blur_sigma)) for d in range(-RADIUS, RADIUS + 1)
)


def gauss(offset, shape, box_dim):
    k = lax.broadcasted_iota(jnp.int32, shape, box_dim)
    p = lax.broadcasted_iota(jnp.int32, shape, 1 - box_dim)
    dist = (offset + k - p).astype(jnp.float32) * (1.0 / S)
    return jnp.exp(dist * dist * (-1.0 / kernel_eps)).astype(jnp.bfloat16)


def blur_weight(d):
    f = d.astype(jnp.float32)
    w = jnp.exp(f * f * (-1.0 / (2.0 * blur_sigma * blur_sigma))) * (1.0 / blur_total)
    return jnp.where(jnp.abs(d) <= RADIUS, w, 0.0)


def split(x):
    hi = x.astype(jnp.bfloat16)
    return hi, (x - hi.astype(jnp.float32)).astype(jnp.bfloat16)


def dot(a, b):
    return jnp.dot(a, b, preferred_element_type=jnp.float32)


def dot_t(a, b):
    return lax.dot_general(a, b, (((1,), (1,)), ((), ())), preferred_element_type=jnp.float32)


def dot_split(a, b):
    (ah, al), (bh, bl) = a, b
    return dot(ah, bh) + (dot(ah, bl) + dot(al, bh))


def bf(x):
    return x.astype(jnp.bfloat16)


def target_of(box_ref, height, width):
    rows = lax.broadcasted_iota(jnp.int32, (BOX, BOX), 0)
    cols = lax.broadcasted_iota(jnp.int32, (BOX, BOX), 1)
    return jnp.where((rows < height) & (cols < width), box_ref[0, 0], 0.0)


MESH = pl.DeviceIdType.MESH
OWN = slice(RADIUS, RADIUS + S)


def tiles(first, count):
    return slice(first * LANES, (first + count) * LANES)


def units_of(per_dev):
    units = [(per_dev - 2, 2 * per_dev, 3)]
    units += [(j, 2 * j + 4, 2) for j in range(per_dev - 3, 0, -1)]
    units += [(0, 2 * per_dev + 3, 1), (0, 0, 3), (0, 3, 3)]
    return units


def kernel(
    per_dev,
    n_row,
    n_col,
    info,
    src,
    box_a,
    box_b,
    out,
    tgt,
    u_loc,
    mv_s,
    mv_u,
    canvas,
    bl,
    r1,
    r2,
    rup,
    cs,
    cl,
    s_send,
    s_recv,
    u_send,
    u_recv,
    x_send,
    x_recv,
    c_send,
    c_recv,
):
    g = pl.program_id(0)
    cols = per_dev * S
    wide = cols + 2 * S
    row, col = lax.axis_index("row"), lax.axis_index("col")
    odd = lax.rem(row, 2) == 1
    even = lax.rem(row, 2) == 0
    units = units_of(per_dev)

    def at(dr, dc):
        return (lax.rem(row + dr + n_row, n_row), lax.rem(col + dc + n_col, n_col))

    def remote(a, b, send, recv, to):
        return pltpu.make_async_remote_copy(
            src_ref=a, dst_ref=b, send_sem=send, recv_sem=recv, device_id=to, device_id_type=MESH
        )

    upper, lower = slice(0, HALF), slice(HALF, S)
    edge = slice(cols - LANES, cols)

    def halo(field, moved, k, send, recv):
        if k == 0:
            a, b, to = field.at[upper, HALF:], moved.at[lower, : cols - HALF], at(-1, 0)
        elif k == 1:
            a, b, to = field.at[upper, :LANES], moved.at[lower, edge], at(-1, -1)
        else:
            a, b, to = field.at[lower, :LANES], moved.at[upper, edge], at(0, -1)
        return remote(a, b, send.at[k], recv.at[k], to)

    def chunk(j):
        lo, hi = max(j * S, HALF), (j + 1) * S
        return remote(
            u_loc.at[upper, lo:hi],
            mv_u.at[lower, lo - HALF : hi - HALF],
            u_send.at[2 + j],
            u_recv.at[2 + j],
            at(-1, 0),
        )

    def corner(k):
        a = u_loc.at[upper, :LANES] if k == 0 else u_loc.at[lower, :LANES]
        b = mv_u.at[lower, edge] if k == 0 else mv_u.at[upper, edge]
        return remote(a, b, u_send.at[k], u_recv.at[k], at(-1, -1) if k == 0 else at(0, -1))

    def spill(n, kind):
        _, first, count = units[n]
        c = tiles(first, count)
        if kind == 0:
            a, b, to = bl.at[RADIUS + S :, c], r1.at[:, c], at(1, 0)
        elif kind == 1:
            a, b, to = bl.at[RADIUS + S : RADIUS + 2 * S, c], r1.at[:S, c], at(1, 0)
        elif kind == 2:
            a, b, to = bl.at[RADIUS + 2 * S :, c], r2.at[:, c], at(2, 0)
        else:
            a, b, to = bl.at[:RADIUS, c], rup.at[:, c], at(-1, 0)
        k = {0: 0, 1: 0, 2: 1, 3: 2}[kind]
        return remote(a, b, x_send.at[n, k], x_recv.at[n, k], to)

    def beside(k):
        if k == 0:
            a, b, to = bl.at[OWN, cols : cols + 3 * LANES], cs.at[:, : 3 * LANES], at(0, 1)
        elif k == 1:
            a, b, to = bl.at[OWN, cols + 3 * LANES :], cs.at[:, 3 * LANES :], at(0, 1)
        else:
            a, b, to = bl.at[OWN, cols + 3 * LANES :], cl, at(0, -1)
        return remote(a, b, c_send.at[k], c_recv.at[k], to)

    sides = 2 if n_col == 2 else 3

    def hand_on(n):
        @pl.when(odd)
        def _():
            c = tiles(units[n][1], units[n][2])
            spill(n, 0).wait_recv()
            bl[RADIUS + S : RADIUS + S + DOWN2, c] += r1[S:, c]
            spill(n, 1).start()
            spill(n, 2).start()

    def give(n):
        spill(n, 3).start()

        @pl.when(even)
        def _():
            spill(n, 0).start()

    def smooth(first, count, band):
        lo, hi = (first - 1) * LANES, (first + count + 1) * LANES
        if lo < 0:
            near = jnp.concatenate([canvas[:, wide + lo :], canvas[:, :hi]], axis=1)
        elif hi > wide:
            near = jnp.concatenate([canvas[:, lo:], canvas[:, : hi - wide]], axis=1)
        else:
            near = canvas[:, lo:hi]
        res = dot_split(split(near), [b[: (count + 2) * LANES, : count * LANES] for b in band])
        if first * LANES + count * LANES > wide:
            bl[:, first * LANES :] = res[:, :LANES]
            bl[:, :LANES] = res[:, LANES:]
        else:
            bl[:, tiles(first, count)] = res

    def the_band():
        n = lax.broadcasted_iota(jnp.int32, (2 * S, S), 0)
        m = lax.broadcasted_iota(jnp.int32, (2 * S, S), 1)
        return split(blur_weight(n - LANES - m))

    def folded(n, dest):
        c = tiles(units[n][1], units[n][2])

        @pl.when(even)
        def _():
            spill(n, 1).wait_recv()
            dest[...] = bl[OWN, c] + r1[:S, c]

        @pl.when(odd)
        def _():
            spill(n, 2).wait_recv()
            mine = bl[OWN, c] + r1[:S, c]
            dest[...] = mine
            dest[:DOWN2] += r2[:, c]

        spill(n, 3).wait_recv()
        dest[S - RADIUS :] += rup[:, c]

    @pl.when(g < per_dev)
    def _():
        barrier = pltpu.get_barrier_semaphore()
        peers = [(-1, 0), (1, 0), (-2, 0), (2, 0), (0, -1), (0, 1), (-1, -1), (1, 1)]

        @pl.when(g == 0)
        def _():
            for dr, dc in peers:
                pl.semaphore_signal(barrier, inc=1, device_id=at(dr, dc), device_id_type=MESH)
            mv_s[upper, : cols - HALF] = src[lower, HALF:]
            canvas[...] = jnp.zeros_like(canvas)

        j = lax.rem(per_dev - g, per_dev)
        o_r, o_c = info[2 * j], info[2 * j + 1]
        h, w = info[2 * per_dev + 2 * j], info[2 * per_dev + 2 * j + 1]
        kr = gauss(o_r, (S, BOX), 1)
        krt = gauss(o_r, (BOX, S), 0)
        kc = gauss(o_c, (S, BOX), 1)
        tgt[...] = target_of(box_a, h, w)
        here = pl.ds(pl.multiple_of(j * S, S), S)
        a = src[:, here]
        in_r = bf(jnp.sum(krt.astype(jnp.float32), axis=1, keepdims=True)).astype(jnp.float32)
        in_c = jnp.sum(kc.astype(jnp.float32), axis=0, keepdims=True)
        back = in_r * in_c
        for step in range(ITERS):
            v = bf(tgt[...] / back)
            u = a / dot_t(bf(dot(kr, v)), kc)
            if step < ITERS - 1:
                back = dot(bf(dot(krt, bf(u))), kc)
        u_loc[:, here] = u

        @pl.when(g == 0)
        def _():
            pl.semaphore_wait(barrier, len(peers))
            for k in range(3):
                halo(src, mv_s, k, s_send, s_recv).start()
            for k in range(2):
                corner(k).start()

        for i in range(per_dev):

            @pl.when(j == i)
            def _():
                chunk(i).start()
                lo, hi = max(i * S, HALF), (i + 1) * S
                mv_u[upper, lo - HALF : hi - HALF] = u_loc[lower, lo:hi]

    @pl.when(g >= per_dev)
    def _():
        j = 2 * per_dev - 1 - g

        @pl.when(j == per_dev - 1)
        def _():
            for k in range(3):
                halo(src, mv_s, k, s_send, s_recv).wait_recv()
            for k in range(2):
                corner(k).wait_recv()

        for i in range(per_dev):

            @pl.when(j == i)
            def _():
                chunk(i).wait_recv()

        base = 4 * per_dev
        o_r, o_c = info[base + 2 * j], info[base + 2 * j + 1]
        h, w = info[base + 2 * per_dev + 2 * j], info[base + 2 * per_dev + 2 * j + 1]
        kr = gauss(o_r, (S, BOX), 1)
        krt = gauss(o_r, (BOX, S), 0)
        kc = gauss(o_c, (S, BOX), 1)
        tgt[...] = target_of(box_b, h, w)
        here = pl.ds(pl.multiple_of(j * S, S), S)
        a = mv_s[:, here]
        u = mv_u[:, here]
        for step in range(ITERS):
            back = dot(bf(dot(krt, bf(u))), kc)
            v = tgt[...] / back
            u = a / dot_t(bf(dot(kr, bf(v))), kc)
            if step == 0:
                for n, (when, _, _) in enumerate(units):
                    if when > 0:

                        @pl.when(j == when - 1)
                        def _():
                            hand_on(n)

        plan = v * dot(bf(dot(krt, bf(u))), kc)

        y = lax.broadcasted_iota(jnp.int32, (TALL, BOX), 0) - RADIUS
        k = lax.broadcasted_iota(jnp.int32, (TALL, BOX), 1)
        rowed = dot_split(split(blur_weight(HALF + o_r + k - y)), split(plan))
        s = HALF + o_c
        lane = lax.broadcasted_iota(jnp.int32, (TALL, LANES), 1)
        turned = [pltpu.roll(rowed[:, tiles(t, 1)], s, 1) for t in range(BOX // LANES)]
        zero = jnp.zeros((TALL, LANES), jnp.float32)
        for t in range(BOX // LANES + 1):
            left = turned[t - 1] if t > 0 else zero
            right = turned[t] if t < BOX // LANES else zero
            spot = pl.ds(pl.multiple_of(j * S + t * LANES, LANES), LANES)
            canvas[:, spot] += jnp.where(lane < s, left, right)

        for n, (when, first, count) in enumerate(units):
            if when > 0:

                @pl.when(j == when)
                def _():
                    band = the_band()
                    for f in range(first, first + count, 2):
                        smooth(f, min(2, first + count - f), band)
                    give(n)

        @pl.when(j == 0)
        def _():
            band = the_band()
            late = [n for n, u_ in enumerate(units) if u_[0] == 0]
            corner_unit, left_unit, right_unit = late
            smooth(2 * per_dev + 3, 2, band)
            give(corner_unit)
            mid = units[left_unit][2]
            last = units[right_unit][1] + units[right_unit][2]
            for f in range(1, mid, 2):
                smooth(f, min(2, mid - f), band)
            give(left_unit)
            hand_on(corner_unit)
            for f in range(mid, last, 2):
                smooth(f, min(2, last - f), band)
            give(right_unit)
            hand_on(left_unit)
            hand_on(right_unit)

            folded(0, bl.at[OWN, tiles(units[0][1], units[0][2])])
            beside(0).start()
            for n in range(1, len(units) - 3):
                folded(n, out.at[:, tiles(units[n][1], units[n][2])])
            folded(corner_unit, bl.at[OWN, tiles(units[corner_unit][1], units[corner_unit][2])])
            for k in range(1, sides):
                beside(k).start()
            folded(left_unit, out.at[:, tiles(units[left_unit][1], units[left_unit][2])])
            folded(right_unit, out.at[:, tiles(units[right_unit][1], units[right_unit][2])])

            ln = lax.broadcasted_iota(jnp.int32, (S, LANES), 1)
            for k in range(sides):
                beside(k).wait_recv()
            out[:, : 3 * LANES] += cs[:, : 3 * LANES]
            out[:, 3 * LANES : 4 * LANES] += jnp.where(ln < LANES - RADIUS, cs[:, 3 * LANES :], 0.0)
            behind = cs[:, 3 * LANES :] if n_col == 2 else cl[...]
            out[:, edge] += jnp.where(ln >= LANES - RADIUS, behind, 0.0)

            for k in range(3):
                halo(src, mv_s, k, s_send, s_recv).wait_send()
            for k in range(2):
                corner(k).wait_send()
            for i in range(per_dev):
                chunk(i).wait_send()
            for k in range(sides):
                beside(k).wait_send()
            for n in range(len(units)):
                spill(n, 3).wait_send()

                @pl.when(even)
                def _():
                    spill(n, 0).wait_send()

                @pl.when(odd)
                def _():
                    spill(n, 1).wait_send()
                    spill(n, 2).wait_send()


def on_device(n_row, n_col, source, boxes_a, shifts_a, widths_a, boxes_b, shifts_b, widths_b):
    cols = source.shape[1]
    per_dev = cols // S
    wide = cols + 2 * S
    units = len(units_of(per_dev))
    info = jnp.concatenate([shifts_a, widths_a, shifts_b, widths_b]).reshape(-1)
    f32 = lambda *shape: pltpu.VMEM(shape, jnp.float32)
    dma = pltpu.SemaphoreType.DMA
    box = (1, 1, BOX, BOX)
    first = lambda g, *_: (0, lax.rem(per_dev - jnp.minimum(g, per_dev - 1), per_dev), 0, 0)
    second = lambda g, *_: (0, jnp.minimum(2 * per_dev - 1 - g, per_dev - 1), 0, 0)
    return pl.pallas_call(
        functools.partial(kernel, per_dev, n_row, n_col),
        grid_spec=pltpu.PrefetchScalarGridSpec(
            num_scalar_prefetch=1,
            grid=(2 * per_dev,),
            in_specs=[
                pl.BlockSpec((S, cols), lambda g, *_: (0, 0)),
                pl.BlockSpec(box, first),
                pl.BlockSpec(box, second),
            ],
            out_specs=pl.BlockSpec((S, cols), lambda g, *_: (0, 0)),
            scratch_shapes=[
                f32(BOX, BOX),
                f32(S, cols),
                f32(S, cols),
                f32(S, cols),
                f32(TALL, wide),
                f32(TALL, wide),
                f32(S + DOWN2, wide),
                f32(DOWN2, wide),
                f32(RADIUS, wide),
                f32(S, 2 * S),
                f32(S, LANES),
                dma((3,)),
                dma((3,)),
                dma((2 + per_dev,)),
                dma((2 + per_dev,)),
                dma((units, 3)),
                dma((units, 3)),
                dma((3,)),
                dma((3,)),
            ],
        ),
        out_shape=jax.ShapeDtypeStruct((S, cols), jnp.float32),
        compiler_params=pltpu.CompilerParams(
            vmem_limit_bytes=56 * 1024 * 1024, collective_id=0, has_side_effects=True
        ),
        name="transport",
    )(info, source, boxes_a, boxes_b)


def solution(mesh):
    return jax.shard_map(
        functools.partial(on_device, mesh.shape["row"], mesh.shape["col"]),
        mesh=mesh,
        in_specs=(
            P("row", "col"),
            P("row", "col", None, None),
            P("row", "col", None),
            P("row", "col", None),
            P("row", "col", None, None),
            P("row", "col", None),
            P("row", "col", None),
        ),
        out_specs=P("row", "col"),
        check_vma=False,
    )
```

```python
import functools
import math

import jax
import jax.numpy as jnp
from jax import lax
from jax.experimental import pallas as pl
from jax.experimental.pallas import tpu as pltpu
from jax.sharding import PartitionSpec as P

S = 256
BOX = 512
ITERS = 3
RADIUS = 8
LANES = 128
HALF = S // 2
DOWN2 = HALF + RADIUS
TALL = RADIUS + 2 * S + DOWN2

kernel_eps = 0.05
blur_sigma = 2.0
blur_total = sum(
    math.exp(-(d * d) / (2.0 * blur_sigma * blur_sigma)) for d in range(-RADIUS, RADIUS + 1)
)


def gauss(offset):
    shape = (LANES, BOX + LANES)
    d = lax.broadcasted_iota(jnp.int32, shape, 1) - lax.broadcasted_iota(jnp.int32, shape, 0)
    g = gauss_of(offset - LANES + d)
    return jnp.concatenate([g[:, LANES:], g[:, :BOX]], axis=0)


def gauss_t(offset):
    shape = (BOX + LANES, LANES)
    d = lax.broadcasted_iota(jnp.int32, shape, 0) - lax.broadcasted_iota(jnp.int32, shape, 1)
    g = gauss_of(offset - LANES + d)
    return jnp.concatenate([g[LANES:], g[:BOX]], axis=1)


def gauss_of(d):
    dist = d.astype(jnp.float32) * (1.0 / S)
    return jnp.exp(dist * dist * (-1.0 / kernel_eps)).astype(jnp.bfloat16)


def blur_weight(d):
    f = d.astype(jnp.float32)
    w = jnp.exp(f * f * (-1.0 / (2.0 * blur_sigma * blur_sigma))) * (1.0 / blur_total)
    return jnp.where(jnp.abs(d) <= RADIUS, w, 0.0)


def split(x):
    hi = x.astype(jnp.bfloat16)
    return hi, (x - hi.astype(jnp.float32)).astype(jnp.bfloat16)


def dot(a, b):
    return jnp.dot(a, b, preferred_element_type=jnp.float32)


def dot_t(a, b):
    return lax.dot_general(a, b, (((1,), (1,)), ((), ())), preferred_element_type=jnp.float32)


def dot_split(a, b):
    (ah, al), (bh, bl) = a, b
    return dot(ah, bh) + (dot(ah, bl) + dot(al, bh))


def bf(x):
    return x.astype(jnp.bfloat16)


def target_of(box_ref, height, width):
    rows = lax.broadcasted_iota(jnp.int32, (BOX, BOX), 0)
    cols = lax.broadcasted_iota(jnp.int32, (BOX, BOX), 1)
    return jnp.where((rows < height) & (cols < width), box_ref[0, 0], 0.0)


MESH = pl.DeviceIdType.MESH
OWN = slice(RADIUS, RADIUS + S)


def tiles(first, count):
    return slice(first * LANES, (first + count) * LANES)


def units_of(per_dev):
    units = [(per_dev - 2, 2 * per_dev, 3)]
    units += [(j, 2 * j + 4, 2) for j in range(per_dev - 3, 0, -1)]
    units += [(0, 2 * per_dev + 3, 1), (0, 0, 3), (0, 3, 3)]
    return units


def kernel(
    per_dev,
    n_row,
    n_col,
    info,
    src,
    box_a,
    box_b,
    out,
    tgt,
    u_loc,
    mv_s,
    mv_u,
    canvas,
    bl,
    band_hi,
    band_lo,
    r1,
    r2,
    rup,
    cs,
    cl,
    s_send,
    s_recv,
    u_send,
    u_recv,
    x_send,
    x_recv,
    c_send,
    c_recv,
):
    g = pl.program_id(0)
    cols = per_dev * S
    wide = cols + 2 * S
    row, col = lax.axis_index("row"), lax.axis_index("col")
    odd = lax.rem(row, 2) == 1
    even = lax.rem(row, 2) == 0
    units = units_of(per_dev)

    def at(dr, dc):
        return (lax.rem(row + dr + n_row, n_row), lax.rem(col + dc + n_col, n_col))

    def remote(a, b, send, recv, to):
        return pltpu.make_async_remote_copy(
            src_ref=a, dst_ref=b, send_sem=send, recv_sem=recv, device_id=to, device_id_type=MESH
        )

    upper, lower = slice(0, HALF), slice(HALF, S)
    edge = slice(cols - LANES, cols)

    def halo(field, moved, k, send, recv):
        if k == 0:
            a, b, to = field.at[upper, HALF:], moved.at[lower, : cols - HALF], at(-1, 0)
        elif k == 1:
            a, b, to = field.at[upper, :LANES], moved.at[lower, edge], at(-1, -1)
        else:
            a, b, to = field.at[lower, :LANES], moved.at[upper, edge], at(0, -1)
        return remote(a, b, send.at[k], recv.at[k], to)

    def chunk(j):
        lo, hi = max(j * S, HALF), (j + 1) * S
        return remote(
            u_loc.at[upper, lo:hi],
            mv_u.at[lower, lo - HALF : hi - HALF],
            u_send.at[2 + j],
            u_recv.at[2 + j],
            at(-1, 0),
        )

    def corner(k):
        a = u_loc.at[upper, :LANES] if k == 0 else u_loc.at[lower, :LANES]
        b = mv_u.at[lower, edge] if k == 0 else mv_u.at[upper, edge]
        return remote(a, b, u_send.at[k], u_recv.at[k], at(-1, -1) if k == 0 else at(0, -1))

    def spill(n, kind):
        _, first, count = units[n]
        c = tiles(first, count)
        if kind == 0:
            a, b, to = bl.at[RADIUS + S :, c], r1.at[:, c], at(1, 0)
        elif kind == 1:
            a, b, to = bl.at[RADIUS + S : RADIUS + 2 * S, c], r1.at[:S, c], at(1, 0)
        elif kind == 2:
            a, b, to = bl.at[RADIUS + 2 * S :, c], r2.at[:, c], at(2, 0)
        else:
            a, b, to = bl.at[:RADIUS, c], rup.at[:, c], at(-1, 0)
        k = {0: 0, 1: 0, 2: 1, 3: 2}[kind]
        return remote(a, b, x_send.at[n, k], x_recv.at[n, k], to)

    def beside(k):
        if k == 0:
            a, b, to = bl.at[OWN, cols : cols + 3 * LANES], cs.at[:, : 3 * LANES], at(0, 1)
        elif k == 1:
            a, b, to = bl.at[OWN, cols + 3 * LANES :], cs.at[:, 3 * LANES :], at(0, 1)
        else:
            a, b, to = bl.at[OWN, cols + 3 * LANES :], cl, at(0, -1)
        return remote(a, b, c_send.at[k], c_recv.at[k], to)

    sides = 2 if n_col == 2 else 3

    def hand_on(n):
        @pl.when(odd)
        def _():
            c = tiles(units[n][1], units[n][2])
            spill(n, 0).wait_recv()
            bl[RADIUS + S : RADIUS + S + DOWN2, c] += r1[S:, c]
            spill(n, 1).start()
            spill(n, 2).start()

    def give(n):
        spill(n, 3).start()

        @pl.when(even)
        def _():
            spill(n, 0).start()

    def smooth(first, count):
        lo, hi = (first - 1) * LANES, (first + count + 1) * LANES
        if lo < 0:
            near = jnp.concatenate([canvas[:, wide + lo :], canvas[:, :hi]], axis=1)
        elif hi > wide:
            near = jnp.concatenate([canvas[:, lo:], canvas[:, : hi - wide]], axis=1)
        else:
            near = canvas[:, lo:hi]
        res = dot_split(split(near), [b[: (count + 2) * LANES, : count * LANES] for b in (band_hi, band_lo)])
        if first * LANES + count * LANES > wide:
            bl[:, first * LANES :] = res[:, :LANES]
            bl[:, :LANES] = res[:, LANES:]
        else:
            bl[:, tiles(first, count)] = res

    def the_band():
        n = lax.broadcasted_iota(jnp.int32, (2 * S, S), 0)
        m = lax.broadcasted_iota(jnp.int32, (2 * S, S), 1)
        return split(blur_weight(n - LANES - m))

    def folded(n, dest):
        c = tiles(units[n][1], units[n][2])

        @pl.when(even)
        def _():
            spill(n, 1).wait_recv()
            dest[...] = bl[OWN, c] + r1[:S, c]

        @pl.when(odd)
        def _():
            spill(n, 2).wait_recv()
            mine = bl[OWN, c] + r1[:S, c]
            dest[...] = mine
            dest[:DOWN2] += r2[:, c]

        spill(n, 3).wait_recv()
        dest[S - RADIUS :] += rup[:, c]

    @pl.when(g < per_dev)
    def _():
        barrier = pltpu.get_barrier_semaphore()
        peers = [(-1, 0), (1, 0), (-2, 0), (2, 0), (0, -1), (0, 1), (-1, -1), (1, 1)]

        @pl.when(g == 0)
        def _():
            for dr, dc in peers:
                pl.semaphore_signal(barrier, inc=1, device_id=at(dr, dc), device_id_type=MESH)
            mv_s[upper, : cols - HALF] = src[lower, HALF:]
            canvas[...] = jnp.zeros_like(canvas)
            band_hi[...], band_lo[...] = the_band()

        j = lax.rem(per_dev - g, per_dev)
        o_r, o_c = info[2 * j], info[2 * j + 1]
        h, w = info[2 * per_dev + 2 * j], info[2 * per_dev + 2 * j + 1]
        kr = gauss(o_r)
        krt = gauss_t(o_r)
        kc = gauss(o_c)
        tgt[...] = target_of(box_a, h, w)
        here = pl.ds(pl.multiple_of(j * S, S), S)
        a = src[:, here]
        in_r = bf(jnp.sum(krt.astype(jnp.float32), axis=1, keepdims=True)).astype(jnp.float32)
        in_c = jnp.sum(kc.astype(jnp.float32), axis=0, keepdims=True)
        back = in_r * in_c
        for step in range(ITERS):
            v = bf(tgt[...] / back)
            u = a / dot_t(bf(dot(kr, v)), kc)
            if step < ITERS - 1:
                back = dot(bf(dot(krt, bf(u))), kc)
        u_loc[:, here] = u

        @pl.when(g == 0)
        def _():
            pl.semaphore_wait(barrier, len(peers))
            for k in range(3):
                halo(src, mv_s, k, s_send, s_recv).start()
            for k in range(2):
                corner(k).start()

        for i in range(per_dev):

            @pl.when(j == i)
            def _():
                chunk(i).start()
                lo, hi = max(i * S, HALF), (i + 1) * S
                mv_u[upper, lo - HALF : hi - HALF] = u_loc[lower, lo:hi]

    @pl.when(g >= per_dev)
    def _():
        j = 2 * per_dev - 1 - g

        @pl.when(j == per_dev - 1)
        def _():
            for k in range(3):
                halo(src, mv_s, k, s_send, s_recv).wait_recv()
            for k in range(2):
                corner(k).wait_recv()

        for i in range(per_dev):

            @pl.when(j == i)
            def _():
                chunk(i).wait_recv()

        base = 4 * per_dev
        o_r, o_c = info[base + 2 * j], info[base + 2 * j + 1]
        h, w = info[base + 2 * per_dev + 2 * j], info[base + 2 * per_dev + 2 * j + 1]
        kr = gauss(o_r)
        krt = gauss_t(o_r)
        kc = gauss(o_c)
        tgt[...] = target_of(box_b, h, w)
        here = pl.ds(pl.multiple_of(j * S, S), S)
        a = mv_s[:, here]
        u = mv_u[:, here]
        for step in range(ITERS):
            back = dot(bf(dot(krt, bf(u))), kc)
            v = tgt[...] / back
            u = a / dot_t(bf(dot(kr, bf(v))), kc)
            if step == 0:
                for n, (when, _, _) in enumerate(units):
                    if when > 0:

                        @pl.when(j == when - 1)
                        def _():
                            hand_on(n)

        plan = v * dot(bf(dot(krt, bf(u))), kc)

        r = lax.broadcasted_iota(jnp.int32, (LANES, 3 * LANES), 0) - RADIUS
        m = lax.broadcasted_iota(jnp.int32, (LANES, 3 * LANES), 1) - 2 * LANES
        weights = split(blur_weight(HALF + o_r + m - r))
        halves = split(plan)
        parts = []
        for b in range(-(-TALL // LANES)):
            height = min(LANES, TALL - b * LANES)
            lo, hi = max(b - 2, 0), min(b + 1, BOX // LANES)
            wt = slice((lo - b + 2) * LANES, (hi - b + 2) * LANES)
            parts.append(
                dot_split(
                    [x[:height, wt] for x in weights],
                    [x[lo * LANES : hi * LANES] for x in halves],
                )
            )
        rowed = jnp.concatenate(parts, axis=0)
        s = HALF + o_c
        lane = lax.broadcasted_iota(jnp.int32, (TALL, LANES), 1)
        turned = [pltpu.roll(rowed[:, tiles(t, 1)], s, 1) for t in range(BOX // LANES)]
        zero = jnp.zeros((TALL, LANES), jnp.float32)
        for t in range(BOX // LANES + 1):
            left = turned[t - 1] if t > 0 else zero
            right = turned[t] if t < BOX // LANES else zero
            spot = pl.ds(pl.multiple_of(j * S + t * LANES, LANES), LANES)
            canvas[:, spot] += jnp.where(lane < s, left, right)

        for n, (when, first, count) in enumerate(units):
            if when > 0:

                @pl.when(j == when)
                def _():
                    for f in range(first, first + count, 2):
                        smooth(f, min(2, first + count - f))
                    give(n)

        @pl.when(j == 0)
        def _():
            late = [n for n, u_ in enumerate(units) if u_[0] == 0]
            corner_unit, left_unit, right_unit = late
            smooth(2 * per_dev + 3, 2)
            give(corner_unit)
            mid = units[left_unit][2]
            last = units[right_unit][1] + units[right_unit][2]
            for f in range(1, mid, 2):
                smooth(f, min(2, mid - f))
            give(left_unit)
            hand_on(corner_unit)
            for f in range(mid, last, 2):
                smooth(f, min(2, last - f))
            give(right_unit)
            hand_on(left_unit)
            hand_on(right_unit)

            folded(0, bl.at[OWN, tiles(units[0][1], units[0][2])])
            beside(0).start()
            for n in range(1, len(units) - 3):
                folded(n, out.at[:, tiles(units[n][1], units[n][2])])
            folded(corner_unit, bl.at[OWN, tiles(units[corner_unit][1], units[corner_unit][2])])
            for k in range(1, sides):
                beside(k).start()
            folded(left_unit, out.at[:, tiles(units[left_unit][1], units[left_unit][2])])
            folded(right_unit, out.at[:, tiles(units[right_unit][1], units[right_unit][2])])

            ln = lax.broadcasted_iota(jnp.int32, (S, LANES), 1)
            for k in range(sides):
                beside(k).wait_recv()
            out[:, : 3 * LANES] += cs[:, : 3 * LANES]
            out[:, 3 * LANES : 4 * LANES] += jnp.where(ln < LANES - RADIUS, cs[:, 3 * LANES :], 0.0)
            behind = cs[:, 3 * LANES :] if n_col == 2 else cl[...]
            out[:, edge] += jnp.where(ln >= LANES - RADIUS, behind, 0.0)

            for k in range(3):
                halo(src, mv_s, k, s_send, s_recv).wait_send()
            for k in range(2):
                corner(k).wait_send()
            for i in range(per_dev):
                chunk(i).wait_send()
            for k in range(sides):
                beside(k).wait_send()
            for n in range(len(units)):
                spill(n, 3).wait_send()

                @pl.when(even)
                def _():
                    spill(n, 0).wait_send()

                @pl.when(odd)
                def _():
                    spill(n, 1).wait_send()
                    spill(n, 2).wait_send()


def on_device(n_row, n_col, source, boxes_a, shifts_a, widths_a, boxes_b, shifts_b, widths_b):
    cols = source.shape[1]
    per_dev = cols // S
    wide = cols + 2 * S
    units = len(units_of(per_dev))
    info = jnp.concatenate([shifts_a, widths_a, shifts_b, widths_b]).reshape(-1)
    f32 = lambda *shape: pltpu.VMEM(shape, jnp.float32)
    dma = pltpu.SemaphoreType.DMA
    box = (1, 1, BOX, BOX)
    first = lambda g, *_: (0, lax.rem(per_dev - jnp.minimum(g, per_dev - 1), per_dev), 0, 0)
    second = lambda g, *_: (0, jnp.minimum(2 * per_dev - 1 - g, per_dev - 1), 0, 0)
    return pl.pallas_call(
        functools.partial(kernel, per_dev, n_row, n_col),
        grid_spec=pltpu.PrefetchScalarGridSpec(
            num_scalar_prefetch=1,
            grid=(2 * per_dev,),
            in_specs=[
                pl.BlockSpec((S, cols), lambda g, *_: (0, 0)),
                pl.BlockSpec(box, first),
                pl.BlockSpec(box, second),
            ],
            out_specs=pl.BlockSpec((S, cols), lambda g, *_: (0, 0)),
            scratch_shapes=[
                f32(BOX, BOX),
                f32(S, cols),
                f32(S, cols),
                f32(S, cols),
                f32(TALL, wide),
                f32(TALL, wide),
                pltpu.VMEM((2 * S, S), jnp.bfloat16),
                pltpu.VMEM((2 * S, S), jnp.bfloat16),
                f32(S + DOWN2, wide),
                f32(DOWN2, wide),
                f32(RADIUS, wide),
                f32(S, 2 * S),
                f32(S, LANES),
                dma((3,)),
                dma((3,)),
                dma((2 + per_dev,)),
                dma((2 + per_dev,)),
                dma((units, 3)),
                dma((units, 3)),
                dma((3,)),
                dma((3,)),
            ],
        ),
        out_shape=jax.ShapeDtypeStruct((S, cols), jnp.float32),
        compiler_params=pltpu.CompilerParams(
            vmem_limit_bytes=56 * 1024 * 1024, collective_id=0, has_side_effects=True
        ),
        name="transport",
    )(info, source, boxes_a, boxes_b)


def solution(mesh):
    return jax.shard_map(
        functools.partial(on_device, mesh.shape["row"], mesh.shape["col"]),
        mesh=mesh,
        in_specs=(
            P("row", "col"),
            P("row", "col", None, None),
            P("row", "col", None),
            P("row", "col", None),
            P("row", "col", None, None),
            P("row", "col", None),
            P("row", "col", None),
        ),
        out_specs=P("row", "col"),
        check_vma=False,
    )
```

```python
import functools
import math

import jax
import jax.numpy as jnp
from jax import lax
from jax.experimental import pallas as pl
from jax.experimental.pallas import tpu as pltpu
from jax.sharding import PartitionSpec as P

S = 256
BOX = 512
ITERS = 3
RADIUS = 8
LANES = 128
HALF = S // 2
DOWN2 = HALF + RADIUS
TALL = RADIUS + 2 * S + DOWN2

kernel_eps = 0.05
blur_sigma = 2.0
blur_total = sum(
    math.exp(-(d * d) / (2.0 * blur_sigma * blur_sigma)) for d in range(-RADIUS, RADIUS + 1)
)


def gauss(offset):
    shape = (LANES, BOX + LANES)
    d = lax.broadcasted_iota(jnp.int32, shape, 1) - lax.broadcasted_iota(jnp.int32, shape, 0)
    g = gauss_of(offset - LANES + d)
    return jnp.concatenate([g[:, LANES:], g[:, :BOX]], axis=0)


def gauss_t(offset):
    shape = (BOX + LANES, LANES)
    d = lax.broadcasted_iota(jnp.int32, shape, 0) - lax.broadcasted_iota(jnp.int32, shape, 1)
    g = gauss_of(offset - LANES + d)
    return jnp.concatenate([g[LANES:], g[:BOX]], axis=1)


def gauss_of(d):
    dist = d.astype(jnp.float32) * (1.0 / S)
    return jnp.exp(dist * dist * (-1.0 / kernel_eps)).astype(jnp.bfloat16)


def blur_weight(d):
    f = d.astype(jnp.float32)
    w = jnp.exp(f * f * (-1.0 / (2.0 * blur_sigma * blur_sigma))) * (1.0 / blur_total)
    return jnp.where(jnp.abs(d) <= RADIUS, w, 0.0)


def split(x):
    hi = x.astype(jnp.bfloat16)
    return hi, (x - hi.astype(jnp.float32)).astype(jnp.bfloat16)


def dot(a, b):
    return jnp.dot(a, b, preferred_element_type=jnp.float32)


def dot_t(a, b):
    return lax.dot_general(a, b, (((1,), (1,)), ((), ())), preferred_element_type=jnp.float32)


def dot_split(a, b):
    (ah, al), (bh, bl) = a, b
    return dot(ah, bh) + (dot(ah, bl) + dot(al, bh))


def bf(x):
    return x.astype(jnp.bfloat16)


def target_of(box_ref, height, width):
    rows = lax.broadcasted_iota(jnp.int32, (BOX, BOX), 0)
    cols = lax.broadcasted_iota(jnp.int32, (BOX, BOX), 1)
    return jnp.where((rows < height) & (cols < width), box_ref[0, 0], 0.0)


MESH = pl.DeviceIdType.MESH
OWN = slice(RADIUS, RADIUS + S)


def tiles(first, count):
    return slice(first * LANES, (first + count) * LANES)


def units_of(per_dev):
    units = [(per_dev - 2, 2 * per_dev, 4)]
    units += [(j, 2 * j + 4, 2) for j in range(per_dev - 3, 1, -1)]
    units += [(1, 5, 3), (0, 2 * per_dev + 4, 1), (0, 0, 3), (0, 3, 2)]
    return units


def kernel(
    per_dev,
    n_row,
    n_col,
    info,
    src,
    box_a,
    box_b,
    out,
    tgt,
    u_loc,
    mv_s,
    mv_u,
    canvas,
    bl,
    band_hi,
    band_lo,
    r1,
    r2,
    rup,
    cs,
    cl,
    s_send,
    s_recv,
    u_send,
    u_recv,
    x_send,
    x_recv,
    c_send,
    c_recv,
):
    g = pl.program_id(0)
    cols = per_dev * S
    wide = cols + 2 * S
    row, col = lax.axis_index("row"), lax.axis_index("col")
    odd = lax.rem(row, 2) == 1
    even = lax.rem(row, 2) == 0
    units = units_of(per_dev)

    def at(dr, dc):
        return (lax.rem(row + dr + n_row, n_row), lax.rem(col + dc + n_col, n_col))

    def remote(a, b, send, recv, to):
        return pltpu.make_async_remote_copy(
            src_ref=a, dst_ref=b, send_sem=send, recv_sem=recv, device_id=to, device_id_type=MESH
        )

    upper, lower = slice(0, HALF), slice(HALF, S)
    edge = slice(cols - LANES, cols)

    def halo(field, moved, k, send, recv):
        if k == 0:
            a, b, to = field.at[upper, HALF:], moved.at[lower, : cols - HALF], at(-1, 0)
        elif k == 1:
            a, b, to = field.at[upper, :LANES], moved.at[lower, edge], at(-1, -1)
        else:
            a, b, to = field.at[lower, :LANES], moved.at[upper, edge], at(0, -1)
        return remote(a, b, send.at[k], recv.at[k], to)

    def chunk(j):
        lo, hi = max(j * S, HALF), (j + 1) * S
        return remote(
            u_loc.at[upper, lo:hi],
            mv_u.at[lower, lo - HALF : hi - HALF],
            u_send.at[2 + j],
            u_recv.at[2 + j],
            at(-1, 0),
        )

    def corner(k):
        a = u_loc.at[upper, :LANES] if k == 0 else u_loc.at[lower, :LANES]
        b = mv_u.at[lower, edge] if k == 0 else mv_u.at[upper, edge]
        return remote(a, b, u_send.at[k], u_recv.at[k], at(-1, -1) if k == 0 else at(0, -1))

    def spill(n, kind):
        _, first, count = units[n]
        c = tiles(first, count)
        if kind == 0:
            a, b, to = bl.at[RADIUS + S :, c], r1.at[:, c], at(1, 0)
        elif kind == 1:
            a, b, to = bl.at[RADIUS + S : RADIUS + 2 * S, c], r1.at[:S, c], at(1, 0)
        elif kind == 2:
            a, b, to = bl.at[RADIUS + 2 * S :, c], r2.at[:, c], at(2, 0)
        else:
            a, b, to = bl.at[:RADIUS, c], rup.at[:, c], at(-1, 0)
        k = {0: 0, 1: 0, 2: 1, 3: 2}[kind]
        return remote(a, b, x_send.at[n, k], x_recv.at[n, k], to)

    def beside(k):
        if k == 0:
            a, b, to = bl.at[OWN, cols:wide], cs, at(0, 1)
        else:
            a, b, to = bl.at[OWN, wide:], cl, at(0, -1)
        return remote(a, b, c_send.at[k], c_recv.at[k], to)

    sides = 2

    def hand_on(n):
        @pl.when(odd)
        def _():
            c = tiles(units[n][1], units[n][2])
            spill(n, 0).wait_recv()
            bl[RADIUS + S : RADIUS + S + DOWN2, c] += r1[S:, c]
            spill(n, 1).start()
            spill(n, 2).start()

    def give(n):
        spill(n, 3).start()

        @pl.when(even)
        def _():
            spill(n, 0).start()

    def smooth(first, count):
        lo, hi = (first - 1) * LANES, (first + count + 1) * LANES
        if lo < 0:
            near = jnp.concatenate([canvas[:, wide + lo :], canvas[:, :hi]], axis=1)
        elif hi > wide:
            near = jnp.concatenate([canvas[:, lo:], canvas[:, : hi - wide]], axis=1)
        else:
            near = canvas[:, lo:hi]
        res = dot_split(split(near), [b[: (count + 2) * LANES, : count * LANES] for b in (band_hi, band_lo)])
        bl[:, tiles(first, count)] = res

    def smooth_edges(right_end):
        near = jnp.concatenate([right_end, jnp.zeros((TALL, LANES), jnp.float32), canvas[:, :LANES]], axis=1)
        band = [b[: 3 * LANES, :LANES] for b in (band_hi, band_lo)]
        bl[:, wide:] = dot_split(split(near), band)

    def the_band():
        n = lax.broadcasted_iota(jnp.int32, (2 * S, S), 0)
        m = lax.broadcasted_iota(jnp.int32, (2 * S, S), 1)
        return split(blur_weight(n - LANES - m))

    def folded(n, dest):
        c = tiles(units[n][1], units[n][2])

        @pl.when(even)
        def _():
            spill(n, 1).wait_recv()
            dest[...] = bl[OWN, c] + r1[:S, c]

        @pl.when(odd)
        def _():
            spill(n, 2).wait_recv()
            mine = bl[OWN, c] + r1[:S, c]
            dest[...] = mine
            dest[:DOWN2] += r2[:, c]

        spill(n, 3).wait_recv()
        dest[S - RADIUS :] += rup[:, c]

    @pl.when(g < per_dev)
    def _():
        barrier = pltpu.get_barrier_semaphore()
        peers = [(-1, 0), (1, 0), (-2, 0), (2, 0), (0, -1), (0, 1), (-1, -1), (1, 1)]

        @pl.when(g == 0)
        def _():
            for dr, dc in peers:
                pl.semaphore_signal(barrier, inc=1, device_id=at(dr, dc), device_id_type=MESH)
            mv_s[upper, : cols - HALF] = src[lower, HALF:]
            canvas[...] = jnp.zeros_like(canvas)
            band_hi[...], band_lo[...] = the_band()

        j = lax.rem(per_dev - g, per_dev)
        o_r, o_c = info[2 * j], info[2 * j + 1]
        h, w = info[2 * per_dev + 2 * j], info[2 * per_dev + 2 * j + 1]
        kr = gauss(o_r)
        krt = gauss_t(o_r)
        kc = gauss(o_c)
        tgt[...] = target_of(box_a, h, w)
        here = pl.ds(pl.multiple_of(j * S, S), S)
        a = src[:, here]
        in_r = bf(jnp.sum(krt.astype(jnp.float32), axis=1, keepdims=True)).astype(jnp.float32)
        in_c = jnp.sum(kc.astype(jnp.float32), axis=0, keepdims=True)
        back = in_r * in_c
        for step in range(ITERS):
            v = bf(tgt[...] / back)
            u = a / dot_t(bf(dot(kr, v)), kc)
            if step < ITERS - 1:
                back = dot(bf(dot(krt, bf(u))), kc)
        u_loc[:, here] = u

        @pl.when(g == 0)
        def _():
            pl.semaphore_wait(barrier, len(peers))
            for k in range(3):
                halo(src, mv_s, k, s_send, s_recv).start()
            for k in range(2):
                corner(k).start()

        for i in range(per_dev):

            @pl.when(j == i)
            def _():
                chunk(i).start()
                lo, hi = max(i * S, HALF), (i + 1) * S
                mv_u[upper, lo - HALF : hi - HALF] = u_loc[lower, lo:hi]

    @pl.when(g >= per_dev)
    def _():
        j = 2 * per_dev - 1 - g

        @pl.when(j == per_dev - 1)
        def _():
            for k in range(3):
                halo(src, mv_s, k, s_send, s_recv).wait_recv()
            for k in range(2):
                corner(k).wait_recv()

        for i in range(per_dev):

            @pl.when(j == i)
            def _():
                chunk(i).wait_recv()

        base = 4 * per_dev
        o_r, o_c = info[base + 2 * j], info[base + 2 * j + 1]
        h, w = info[base + 2 * per_dev + 2 * j], info[base + 2 * per_dev + 2 * j + 1]
        kr = gauss(o_r)
        krt = gauss_t(o_r)
        kc = gauss(o_c)
        tgt[...] = target_of(box_b, h, w)
        here = pl.ds(pl.multiple_of(j * S, S), S)
        a = mv_s[:, here]
        u = mv_u[:, here]
        for step in range(ITERS):
            back = dot(bf(dot(krt, bf(u))), kc)
            v = tgt[...] / back
            u = a / dot_t(bf(dot(kr, bf(v))), kc)
            if step == 0:
                for n, (when, _, _) in enumerate(units):
                    if when > 0:

                        @pl.when(j == when - 1)
                        def _():
                            hand_on(n)

        plan = v * dot(bf(dot(krt, bf(u))), kc)

        r = lax.broadcasted_iota(jnp.int32, (LANES, 3 * LANES), 0) - RADIUS
        m = lax.broadcasted_iota(jnp.int32, (LANES, 3 * LANES), 1) - 2 * LANES
        weights = split(blur_weight(HALF + o_r + m - r))
        halves = split(plan)
        parts = []
        for b in range(-(-TALL // LANES)):
            height = min(LANES, TALL - b * LANES)
            lo, hi = max(b - 2, 0), min(b + 1, BOX // LANES)
            wt = slice((lo - b + 2) * LANES, (hi - b + 2) * LANES)
            parts.append(
                dot_split(
                    [x[:height, wt] for x in weights],
                    [x[lo * LANES : hi * LANES] for x in halves],
                )
            )
        rowed = jnp.concatenate(parts, axis=0)
        s = HALF + o_c
        lane = lax.broadcasted_iota(jnp.int32, (TALL, LANES), 1)
        turned = [pltpu.roll(rowed[:, tiles(t, 1)], s, 1) for t in range(BOX // LANES)]
        zero = jnp.zeros((TALL, LANES), jnp.float32)
        for t in range(BOX // LANES + 1):
            left = turned[t - 1] if t > 0 else zero
            right = turned[t] if t < BOX // LANES else zero
            spot = pl.ds(pl.multiple_of(j * S + t * LANES, LANES), LANES)
            piece = jnp.where(lane < s, left, right)
            canvas[:, spot] += piece

        for n, (when, first, count) in enumerate(units):
            if when > 0:

                @pl.when(j == when)
                def _():
                    for f in range(first, first + count, 2):
                        smooth(f, min(2, first + count - f))
                    give(n)

        @pl.when(j == 0)
        def _():
            late = [n for n, u_ in enumerate(units) if u_[0] == 0]
            corner_unit, left_unit, right_unit = late
            smooth_edges(piece)
            give(corner_unit)
            mid = units[left_unit][2]
            last = units[right_unit][1] + units[right_unit][2]
            for f in range(0, mid, 2):
                smooth(f, min(2, mid - f))
            give(left_unit)
            hand_on(corner_unit)
            for f in range(mid, last, 2):
                smooth(f, min(2, last - f))
            give(right_unit)
            hand_on(left_unit)
            hand_on(right_unit)

            folded(0, bl.at[OWN, tiles(units[0][1], units[0][2])])
            beside(0).start()
            for n in range(1, len(units) - 3):
                folded(n, out.at[:, tiles(units[n][1], units[n][2])])
            folded(corner_unit, bl.at[OWN, tiles(units[corner_unit][1], units[corner_unit][2])])
            for k in range(1, sides):
                beside(k).start()
            folded(left_unit, out.at[:, tiles(units[left_unit][1], units[left_unit][2])])
            folded(right_unit, out.at[:, tiles(units[right_unit][1], units[right_unit][2])])

            ln = lax.broadcasted_iota(jnp.int32, (S, LANES), 1)
            for k in range(sides):
                beside(k).wait_recv()
            out[:, : 4 * LANES] += cs[...]
            out[:, tiles(5, 1)] += jnp.where(ln < RADIUS, bl[OWN, wide:], 0.0)
            out[:, edge] += jnp.where(ln >= LANES - RADIUS, cl[...], 0.0)

            for k in range(3):
                halo(src, mv_s, k, s_send, s_recv).wait_send()
            for k in range(2):
                corner(k).wait_send()
            for i in range(per_dev):
                chunk(i).wait_send()
            for k in range(sides):
                beside(k).wait_send()
            for n in range(len(units)):
                spill(n, 3).wait_send()

                @pl.when(even)
                def _():
                    spill(n, 0).wait_send()

                @pl.when(odd)
                def _():
                    spill(n, 1).wait_send()
                    spill(n, 2).wait_send()


def on_device(n_row, n_col, source, boxes_a, shifts_a, widths_a, boxes_b, shifts_b, widths_b):
    cols = source.shape[1]
    per_dev = cols // S
    wide = cols + 2 * S
    units = len(units_of(per_dev))
    info = jnp.concatenate([shifts_a, widths_a, shifts_b, widths_b]).reshape(-1)
    f32 = lambda *shape: pltpu.VMEM(shape, jnp.float32)
    dma = pltpu.SemaphoreType.DMA
    box = (1, 1, BOX, BOX)
    first = lambda g, *_: (0, lax.rem(per_dev - jnp.minimum(g, per_dev - 1), per_dev), 0, 0)
    second = lambda g, *_: (0, jnp.minimum(2 * per_dev - 1 - g, per_dev - 1), 0, 0)
    return pl.pallas_call(
        functools.partial(kernel, per_dev, n_row, n_col),
        grid_spec=pltpu.PrefetchScalarGridSpec(
            num_scalar_prefetch=1,
            grid=(2 * per_dev,),
            in_specs=[
                pl.BlockSpec((S, cols), lambda g, *_: (0, 0)),
                pl.BlockSpec(box, first),
                pl.BlockSpec(box, second),
            ],
            out_specs=pl.BlockSpec((S, cols), lambda g, *_: (0, 0)),
            scratch_shapes=[
                f32(BOX, BOX),
                f32(S, cols),
                f32(S, cols),
                f32(S, cols),
                f32(TALL, wide),
                f32(TALL, wide + LANES),
                pltpu.VMEM((2 * S, S), jnp.bfloat16),
                pltpu.VMEM((2 * S, S), jnp.bfloat16),
                f32(S + DOWN2, wide + LANES),
                f32(DOWN2, wide + LANES),
                f32(RADIUS, wide + LANES),
                f32(S, 2 * S),
                f32(S, LANES),
                dma((3,)),
                dma((3,)),
                dma((2 + per_dev,)),
                dma((2 + per_dev,)),
                dma((units, 3)),
                dma((units, 3)),
                dma((3,)),
                dma((3,)),
            ],
        ),
        out_shape=jax.ShapeDtypeStruct((S, cols), jnp.float32),
        compiler_params=pltpu.CompilerParams(
            vmem_limit_bytes=56 * 1024 * 1024, collective_id=0, has_side_effects=True
        ),
        name="transport",
    )(info, source, boxes_a, boxes_b)


def solution(mesh):
    return jax.shard_map(
        functools.partial(on_device, mesh.shape["row"], mesh.shape["col"]),
        mesh=mesh,
        in_specs=(
            P("row", "col"),
            P("row", "col", None, None),
            P("row", "col", None),
            P("row", "col", None),
            P("row", "col", None, None),
            P("row", "col", None),
            P("row", "col", None),
        ),
        out_specs=P("row", "col"),
        check_vma=False,
    )
```
